256 devices in a mesh: seq: 32 (over y, z), head: 8 (over x, core).
Axes of the slice: x: 4, y: 4, z: 8, core: 2. Of those that a mesh axis runs over, the one named last changes fastest.
Arguments:
- block_input: bfloat16 [4096, 3072], P('seq'), may hold values from -12 to 12
- grad_output: bfloat16 [4096, 3072], P('seq'), may hold values from -6 to 6
- weights: bfloat16 [3072, 4, 3072], P('seq', None, 'head'), may hold values from -0.109375 to 0.109375
- clip_ids: int32 [32], replicated, may hold values from 0 to 2, never falling along the last dimension, each value on 1 to 16 neighbouring positions
Outputs:
- grad_input: bfloat16 [4096, 3072], P('seq', 'head')
- grad_weights: bfloat16 [3072, 4, 3072], P('seq', None, 'head')
The draws below stay inside these ranges and needn't reach their ends.
Inputs may be any that keep to these rules, and one draw needn't show every extreme that they name: `clip_ids`: clip numbers never fall from one frame to the next; every clip number of 0 to 2 is used, each clip spans 1 to 16 frames and one spans exactly 16.
All inputs are finite; a program needn't handle non-finite values.
Results may differ from the reference program's by a relative error of at most 0.018.
Values may be sent and summed in bfloat16 or wider, within the bound.
No kernel may reach another device: no remote copies, remote signals or barrier semaphores. Data moves between devices by JAX's collectives and lax.ppermute only.
A program may use at most 128 MiB of HBM per device.

```python
import math
import jax
import jax.numpy as jnp
import numpy as np
from jax import lax

D = 3072
HD = 128
WIN = 1
P_SIZE = 128
F_DEV = 1
HH = 3072
FRAMES = 32
TOKENS = 4096
CLIPS = 3
MOST_FRAMES = 16
N_HEAD = 8


def draw_block_input(key, part):
    base_draw = jnp.clip(jax.random.normal(key, (TOKENS, D), jnp.float32), -6.0, 6.0)
    return base_draw.astype(jnp.bfloat16)


def with_spikes(values, stream_key, source, target, parts, factor):
    owner, partner = [(jnp.arange(values.shape[axis_at]) // (values.shape[axis_at] // parts)).reshape([-1 if axis == axis_at else 1 for axis in range(values.ndim)]) for axis_at in (source, target)]
    chosen = jax.random.permutation(stream_key, parts)[partner]
    strong = (owner == chosen) | (owner == (partner + parts // 2) % parts)
    return jnp.where(strong, factor * values, values)


def level_of(own_key, dims, pieces, smallest, high):
    def one(position, shards_of):
        steps = jax.random.uniform(jax.random.fold_in(jax.random.fold_in(own_key, 6), position), (shards_of,), jnp.float32, smallest / len(pieces), high / len(pieces))
        return jnp.repeat(jnp.exp(steps), dims[position] // shards_of).reshape((-1,) + (1,) * (len(dims) - position - 1))

    level = one(*pieces[0])
    for cut in pieces[1:]:
        level = level * one(*cut)
    return level


def profile(amount, total, bound, slope):
    weights = [(1 << 20) // math.isqrt(standing ** slope) + 1 for standing in range(2, amount + 1)]
    spare, holding = total - bound - (amount - 1), [1] * (amount - 1)
    while spare > 0:
        free = [i for i in range(amount - 1) if holding[i] < bound]
        pool, left = sum([weights[i] for i in free]), spare
        for i in free:
            addition = min(bound - holding[i], max(1, left * weights[i] // pool), spare)
            holding[i] = holding[i] + addition
            spare = spare - addition
    return np.array([bound] + holding)


def uneven(own_key, amount, total, reach, skew):
    if amount == 2:
        one = jax.random.randint(own_key, (), max(1, total - reach), min(reach, total - 1) + 1)
        return jnp.stack([one, total - one])
    tallies = jnp.asarray(profile(amount, total, reach, skew), jnp.int32)
    twos = (amount - 1) // 2
    source_of, taker = tallies[1:1 + 2 * twos:2], tallies[2:2 + 2 * twos:2]
    margin = jnp.minimum(source_of - 1, reach - taker)
    shifted = jax.random.randint(jax.random.fold_in(own_key, 1), (twos,), 0, 1 << 20) % (margin + 1)
    tallies = tallies.at[1:1 + 2 * twos:2].set(source_of - shifted).at[2:2 + 2 * twos:2].set(taker + shifted)
    return tallies[jax.random.permutation(jax.random.fold_in(own_key, 2), amount)]


def noise(stream_key, dims, deviation, limit, pieces=(), kind=jnp.bfloat16):
    entries = jax.random.normal(stream_key, dims, jnp.float32) * deviation
    if len(pieces) > 0:
        entries = level_of(stream_key, dims, pieces, -0.22, 0.18) * entries
    return jnp.clip(entries, min=-limit, max=limit).astype(kind)


def noise_with(rng, extent, deviation, bound, shards, heavy, kind=jnp.bfloat16):
    array = deviation * jax.random.normal(rng, extent, jnp.float32)
    if shards:
        array = array * level_of(rng, extent, shards, -0.22, 0.18)
    return jnp.clip(with_spikes(array, jax.random.fold_in(rng, 3), *heavy), -bound, bound).astype(kind)


def setup_inputs(seed: int = 0) -> dict:
    keys = jax.random.split(jax.random.key(seed), 5)
    return {
        "block_input": draw_block_input(jax.random.fold_in(keys[4], 71), 0),
        "grad_output": noise_with(keys[1], (TOKENS, D), 1.0, 6.0, ((0, 32),), (0, 1, 32, 2.75)),
        "weights": noise(keys[2], (D, 4, HH), D ** -0.5, 0.109375, ((0, 32), (2, 8))),
        "clip_ids": jnp.searchsorted(jnp.cumsum(uneven(keys[3], CLIPS, FRAMES, MOST_FRAMES, 1)), jnp.arange(FRAMES), side="right").astype(jnp.int32),
    }


big_negative = -1.0e30


def attend(query_rows, key_ext, value_ext, grad_rows, clip_ext):
    frame_count = clip_ext.shape[0] - 2 * WIN
    window_len = 2 * WIN + 1
    head_count = query_rows.shape[1] // HD
    score_scale = HD ** -0.5
    query_frames = query_rows.reshape(frame_count, P_SIZE, head_count, HD).astype(jnp.float32)
    key_frames = key_ext.reshape(frame_count + 2 * WIN, P_SIZE, head_count, HD)
    value_frames = value_ext.reshape(frame_count + 2 * WIN, P_SIZE, head_count, HD)
    grad_frames = grad_rows.reshape(frame_count, P_SIZE, head_count, HD).astype(jnp.float32)
    key_window = jnp.stack([key_frames[offset:offset + frame_count] for offset in range(window_len)], axis=1).astype(jnp.float32)
    value_window = jnp.stack([value_frames[offset:offset + frame_count] for offset in range(window_len)], axis=1).astype(jnp.float32)
    clip_window = jnp.stack([clip_ext[offset:offset + frame_count] for offset in range(window_len)], axis=1)
    allowed = clip_window == clip_ext[WIN:WIN + frame_count][:, None]
    allowed = allowed[:, None, None, :, None]
    scores = jnp.einsum("fihc,fojhc->fhioj", query_frames, key_window) * score_scale
    masked = jnp.where(allowed, scores, big_negative)
    top_score = jnp.max(masked, axis=(3, 4), keepdims=True)
    expo_terms = jnp.where(allowed, jnp.exp(masked - top_score), 0.0)
    attn_prob = expo_terms / jnp.sum(expo_terms, axis=(3, 4), keepdims=True)
    prob_low = attn_prob.astype(jnp.bfloat16).astype(jnp.float32)
    attn_out = jnp.einsum("fhioj,fojhc->fihc", prob_low, value_window)
    delta_row = jnp.sum(grad_frames * attn_out, axis=3)
    delta_row = jnp.transpose(delta_row, (0, 2, 1))[:, :, :, None, None]
    grad_prob = jnp.einsum("fihc,fojhc->fhioj", grad_frames, value_window)
    grad_score = (attn_prob * (grad_prob - delta_row)).astype(jnp.bfloat16).astype(jnp.float32)
    grad_query = jnp.einsum("fhioj,fojhc->fihc", grad_score, key_window) * score_scale
    grad_key_window = jnp.einsum("fhioj,fihc->fojhc", grad_score, query_frames) * score_scale
    grad_value_window = jnp.einsum("fhioj,fihc->fojhc", prob_low, grad_frames)
    grad_key = jnp.zeros((frame_count + 2 * WIN, P_SIZE, head_count, HD), jnp.float32)
    grad_value = jnp.zeros((frame_count + 2 * WIN, P_SIZE, head_count, HD), jnp.float32)
    for offset in range(window_len):
        grad_key = grad_key.at[offset:offset + frame_count].add(grad_key_window[:, offset])
        grad_value = grad_value.at[offset:offset + frame_count].add(grad_value_window[:, offset])
    column_count = head_count * HD
    return (grad_query.reshape(frame_count * P_SIZE, column_count),
            grad_key.reshape((frame_count + 2 * WIN) * P_SIZE, column_count),
            grad_value.reshape((frame_count + 2 * WIN) * P_SIZE, column_count),
            attn_out.astype(jnp.bfloat16).reshape(frame_count * P_SIZE, column_count))


def reference(block_input, grad_output, weights, clip_ids):
    token_count = block_input.shape[0]
    feature_count = block_input.shape[1]
    column_count = weights.shape[2]
    qkv_weights = weights[:, :3].reshape(feature_count, 3 * column_count)
    projected = jnp.dot(block_input, qkv_weights, preferred_element_type=jnp.float32).astype(jnp.bfloat16)
    grad_attn = jnp.dot(grad_output, weights[:, 3], preferred_element_type=jnp.float32).astype(jnp.bfloat16)
    query_all = projected[:, :column_count]
    key_all = projected[:, column_count:2 * column_count]
    value_all = projected[:, 2 * column_count:]
    rim_rows = WIN * P_SIZE
    group_rows = F_DEV * P_SIZE
    group_count = token_count // group_rows
    rim_zeros = jnp.zeros((rim_rows, column_count), jnp.bfloat16)
    key_padded = jnp.concatenate([rim_zeros, key_all, rim_zeros], axis=0)
    value_padded = jnp.concatenate([rim_zeros, value_all, rim_zeros], axis=0)
    clip_rim = jnp.full((WIN,), -1, jnp.int32)
    clip_padded = jnp.concatenate([clip_rim, clip_ids.astype(jnp.int32), clip_rim])
    span_rows = group_rows + 2 * rim_rows

    def one_group(running, group_index):
        grad_key_pad, grad_value_pad = running
        row_start = (group_index * group_rows).astype(jnp.int32)
        query_rows = lax.dynamic_slice_in_dim(query_all, row_start, group_rows, 0)
        key_ext = lax.dynamic_slice_in_dim(key_padded, row_start, span_rows, 0)
        value_ext = lax.dynamic_slice_in_dim(value_padded, row_start, span_rows, 0)
        grad_rows = lax.dynamic_slice_in_dim(grad_attn, row_start, group_rows, 0)
        clip_ext = lax.dynamic_slice_in_dim(clip_padded, (group_index * F_DEV).astype(jnp.int32), F_DEV + 2 * WIN, 0)
        grad_query, grad_key, grad_value, attn_low = attend(query_rows, key_ext, value_ext, grad_rows, clip_ext)
        grad_key_pad = lax.dynamic_update_slice_in_dim(
            grad_key_pad, lax.dynamic_slice_in_dim(grad_key_pad, row_start, span_rows, 0) + grad_key, row_start, 0)
        grad_value_pad = lax.dynamic_update_slice_in_dim(
            grad_value_pad, lax.dynamic_slice_in_dim(grad_value_pad, row_start, span_rows, 0) + grad_value, row_start, 0)
        return (grad_key_pad, grad_value_pad), (grad_query, attn_low)

    zero_pad = jnp.zeros((token_count + 2 * rim_rows, column_count), jnp.float32)
    (grad_key_pad, grad_value_pad), (grad_query, attn_low) = lax.scan(
        one_group, (zero_pad, zero_pad), jnp.arange(group_count, dtype=jnp.int32))
    grad_query = grad_query.reshape(token_count, column_count)
    attn_low = attn_low.reshape(token_count, column_count)
    grad_qkv = jnp.concatenate([grad_query, grad_key_pad[rim_rows:rim_rows + token_count],
                                grad_value_pad[rim_rows:rim_rows + token_count]], axis=1).astype(jnp.bfloat16)

    head_groups = N_HEAD
    group_cols = column_count // head_groups
    grad_split = grad_qkv.reshape(token_count, 3, head_groups, group_cols)
    weight_split = weights[:, :3].reshape(feature_count, 3, head_groups, group_cols)

    def head_part(running, head_index):
        grad_piece = lax.dynamic_index_in_dim(grad_split, head_index, 2, keepdims=False).reshape(token_count, 3 * group_cols)
        weight_piece = lax.dynamic_index_in_dim(weight_split, head_index, 2, keepdims=False).reshape(feature_count, 3 * group_cols)
        partial_term = lax.dot_general(grad_piece, weight_piece, (((1,), (1,)), ((), ())), preferred_element_type=jnp.float32)
        rounded = lax.optimization_barrier(partial_term.astype(jnp.bfloat16)).astype(jnp.float32)
        return running + rounded, None

    grad_input, unused = lax.scan(head_part, jnp.zeros((token_count, feature_count), jnp.float32),
                                  jnp.arange(head_groups, dtype=jnp.int32))

    def seq_part(running, group_index):
        row_start = (group_index * group_rows).astype(jnp.int32)
        input_rows = lax.dynamic_slice_in_dim(block_input, row_start, group_rows, 0)
        output_rows = lax.dynamic_slice_in_dim(grad_output, row_start, group_rows, 0)
        qkv_rows = lax.dynamic_slice_in_dim(grad_qkv, row_start, group_rows, 0)
        attn_rows = lax.dynamic_slice_in_dim(attn_low, row_start, group_rows, 0)
        qkv_term = lax.dot_general(input_rows, qkv_rows, (((0,), (0,)), ((), ())),
                                   preferred_element_type=jnp.float32).reshape(feature_count, 3, column_count)
        out_term = lax.dot_general(output_rows, attn_rows, (((0,), (0,)), ((), ())),
                                   preferred_element_type=jnp.float32)[:, None, :]
        term_all = jnp.concatenate([qkv_term, out_term], axis=1)
        rounded = lax.optimization_barrier(term_all.astype(jnp.bfloat16)).astype(jnp.float32)
        return running + rounded, None

    grad_weights, unused_two = lax.scan(seq_part, jnp.zeros((feature_count, 4, column_count), jnp.float32),
                                        jnp.arange(group_count, dtype=jnp.int32))
    return grad_input.astype(jnp.bfloat16), grad_weights.astype(jnp.bfloat16)
```

```python
import functools

import jax
import jax.numpy as jnp
from jax import lax
from jax.experimental import pallas as pl
from jax.experimental.pallas import tpu as pltpu
from jax.sharding import Mesh
from jax.sharding import PartitionSpec as P

F32 = jnp.float32
BF16 = jnp.bfloat16
HD = 128
NY, NZ, NX = 4, 8, 4
TOK = 128
COLS = 384
BLK = 768
SLAB = 96


VM = pl.BlockSpec(memory_space=pltpu.VMEM)
ANY = pl.BlockSpec(memory_space=pl.ANY)
SM = pl.BlockSpec(memory_space=pltpu.SMEM)


def sds(shape, dtype):
    return jax.ShapeDtypeStruct(shape, dtype)


def mm(a, b, ca, cb):
    return lax.dot_general(a, b, (((ca,), (cb,)), ((), ())), preferred_element_type=F32)


def cyc(n, k):
    return [(i, (i + k) % n) for i in range(n)]


def params():
    return pltpu.CompilerParams(vmem_limit_bytes=48 * 2**20)


def gather_weights(refs, wfull):
    z = lax.axis_index("z")
    for j, ref in enumerate(refs):
        shift = -j if j <= 4 else j - 4
        start = pl.multiple_of(lax.rem(z + shift + NZ, NZ) * SLAB, 32)
        wfull[:, pl.ds(start, SLAB), :] = ref[...]


def put_partials(part, s, outs):
    outs[0][:, s * COLS : (s + 1) * COLS] = part[:TOK]
    for k in range(1, NY):
        outs[k][:, s * COLS : (s + 1) * COLS] = part[k * TOK : (k + 1) * TOK].astype(BF16)


def proj_kv_body(x_hbm, *refs):
    t, o, w = refs[0:3], refs[3:6], refs[6:14]
    outs, xt, wfull, sem = refs[14:18], refs[18], refs[19], refs[20]
    y, c = lax.axis_index("y"), lax.axis_index("c")
    own = pltpu.make_async_copy(
        x_hbm.at[:, pl.ds(pl.multiple_of(y * BLK, BLK), BLK)], xt.at[pl.ds(0, TOK), :], sem
    )
    own.start()
    gather_weights(w, wfull)
    for k in range(1, NY):
        xt[k * TOK : (k + 1) * TOK, :] = jnp.where(c == 0, t[k - 1][...], o[k - 1][...])
    own.wait()
    rows = xt[...]
    for s in range(2):
        put_partials(mm(rows, wfull[s], 1, 0), s, outs)


def proj_qo_body(g_hbm, xt, *refs):
    t, o, w = refs[0:3], refs[3:6], refs[6:14]
    outs, gt, wfull, sem = refs[14:18], refs[18], refs[19], refs[20]
    y, c = lax.axis_index("y"), lax.axis_index("c")
    own = pltpu.make_async_copy(
        g_hbm.at[:, pl.ds(pl.multiple_of(y * BLK, BLK), BLK)], gt.at[pl.ds(0, TOK), :], sem
    )
    own.start()
    gather_weights(w, wfull)
    for k in range(1, NY):
        gt[k * TOK : (k + 1) * TOK, :] = jnp.where(c == 0, o[k - 1][...], t[k - 1][...])
    put_partials(mm(xt[...], wfull[0], 1, 0), 0, outs)
    own.wait()
    put_partials(mm(gt[...], wfull[1], 1, 0), 1, outs)


def attend_body(clip, kv, kv_lo, kv_hi, own, r1, r2, r3, out_qa, out_own, out_lo, out_hi):
    s_idx = lax.axis_index("y") * NZ + lax.axis_index("z")
    last = NY * NZ - 1
    mine = clip[s_idx]
    ok_lo = jnp.logical_and(s_idx > 0, clip[jnp.maximum(s_idx - 1, 0)] == mine)
    ok_hi = jnp.logical_and(s_idx < last, clip[jnp.minimum(s_idx + 1, last)] == mine)
    col = lax.broadcasted_iota(jnp.int32, (TOK, 3 * TOK), 1)
    allowed = jnp.where(
        col < TOK,
        ok_lo.astype(jnp.int32),
        jnp.where(col < 2 * TOK, 1, ok_hi.astype(jnp.int32)),
    ) > 0
    scale = HD**-0.5
    qg = (
        own[...] + r1[...].astype(F32) + r2[...].astype(F32) + r3[...].astype(F32)
    ).astype(BF16)
    for h in range(3):
        a, b = h * HD, COLS + h * HD
        q, g = qg[:, a : a + HD], qg[:, b : b + HD]
        k3 = jnp.concatenate([r[:, a : a + HD] for r in (kv_lo, kv, kv_hi)], axis=0)
        v3 = jnp.concatenate([r[:, b : b + HD] for r in (kv_lo, kv, kv_hi)], axis=0)
        scores = jnp.where(allowed, mm(q, k3, 1, 1) * scale, -1e30)
        top = jnp.max(scores, axis=1, keepdims=True)
        expo = jnp.where(allowed, jnp.exp(scores - top), 0.0)
        prob = expo / jnp.sum(expo, axis=1, keepdims=True)
        low = prob.astype(BF16)
        attn = mm(low, v3, 1, 0)
        delta = jnp.sum(g.astype(F32) * attn, axis=1, keepdims=True)
        ds = (prob * (mm(g, v3, 1, 1) - delta)).astype(BF16)
        out_qa[:, a : a + HD] = (mm(ds, k3, 1, 0) * scale).astype(BF16)
        out_qa[:, b : b + HD] = attn.astype(BF16)
        gk = mm(ds, q, 0, 0) * scale
        gv = mm(low, g, 0, 0)
        for at, val in ((a, gk), (b, gv)):
            out_lo[:, at : at + HD] = val[:TOK].astype(BF16)
            out_own[:, at : at + HD] = val[TOK : 2 * TOK]
            out_hi[:, at : at + HD] = val[2 * TOK :].astype(BF16)


def weight_grad_body(left, right, g0, g1, g2, g3, *refs):
    outs, acc = refs[:NZ], refs[NZ]
    z = lax.axis_index("z")
    for s, rows in enumerate((left, right)):
        cols = jnp.concatenate([r[:, s * COLS : (s + 1) * COLS] for r in (g0, g1, g2, g3)], axis=0)
        acc[s] = mm(rows[...], cols, 0, 0)
    for j in range(NZ):
        start = pl.multiple_of(lax.rem(z + j, NZ) * SLAB, 32)
        outs[j][...] = acc[:, pl.ds(start, SLAB), :].astype(outs[j].dtype)


def input_grad_body(wkv, wqo, *refs):
    qa, kv = refs[0:4], refs[4:8]
    keep, send, acc = refs[8], refs[9], refs[10]
    y, x, c = lax.axis_index("y"), lax.axis_index("x"), lax.axis_index("c")
    q = jnp.concatenate([r[:, :COLS] for r in qa], axis=0)
    k = jnp.concatenate([r[:, :COLS] for r in kv], axis=0)
    v = jnp.concatenate([r[:, COLS:] for r in kv], axis=0)
    for half in range(2):
        d = pl.ds(half * COLS, COLS)
        total = mm(q, wqo[0, d, :], 1, 1) + mm(k, wkv[0, d, :], 1, 1) + mm(v, wkv[1, d, :], 1, 1)
        for b in range(NY):
            acc[half, b] = total[b * TOK : (b + 1) * TOK]
    for j in range(NY):
        b = lax.rem(y - x - j + 3 * NY, NY)
        keep[j] = acc[c, b]
        send[j] = acc[1 - c, b].astype(BF16)


def call(body, ins, specs, outs, scratch=()):
    return pl.pallas_call(
        body,
        in_specs=specs,
        out_specs=[VM] * len(outs),
        out_shape=[sds(*o) for o in outs],
        scratch_shapes=list(scratch),
        compiler_params=params(),
    )(*ins)


def z_gather(w):
    right, left = [w], []
    for k in range(4):
        right.append(lax.ppermute(right[-1], "z", cyc(NZ, 1)))
        if k < 3:
            left.append(lax.ppermute(left[-1] if left else w, "z", cyc(NZ, -1)))
    return right + left


def add(a, b):
    return (a.astype(F32) + b.astype(F32)).astype(BF16)


def z_reduce(slabs):
    up, down = slabs[4], slabs[5]
    for k in range(4):
        up = lax.ppermute(up, "z", cyc(NZ, 1))
        if k < 3:
            up = add(up, slabs[3 - k])
            down = lax.ppermute(down, "z", cyc(NZ, -1))
            if k < 2:
                down = add(down, slabs[6 + k])
    return (slabs[0] + up.astype(F32) + down.astype(F32)).astype(BF16)


def y_reduce(parts):
    return [lax.ppermute(parts[k], "y", cyc(NY, -k)) for k in range(1, NY)]


def y_gather(rows):
    return [rows] + [lax.ppermute(rows, "y", cyc(NY, k)) for k in range(1, NY)]


def on_device(block_input, grad_output, weights, clip_ids):
    y, c = lax.axis_index("y"), lax.axis_index("c")
    frames = NY * NZ
    ahead = [(i, i + 1) for i in range(frames - 1)]
    behind = [(i + 1, i) for i in range(frames - 1)]
    w_kv = jnp.transpose(weights[:, 1:3], (1, 0, 2))
    w_qo = jnp.transpose(weights[:, 0::3], (1, 0, 2))
    kv_pieces = z_gather(w_kv)
    t = []
    for k in range(1, NY):
        start = lax.rem(y + k, NY) * BLK
        piece = jnp.where(
            c == 0,
            lax.dynamic_slice_in_dim(block_input, start, BLK, 1),
            lax.dynamic_slice_in_dim(grad_output, start, BLK, 1),
        )
        t.append(lax.ppermute(piece, "y", cyc(NY, k)))
    o = [lax.ppermute(piece, "c", cyc(2, 1)) for piece in t]
    qo_pieces = z_gather(w_qo)

    part_shapes = [((TOK, BLK), F32)] + [((TOK, BLK), BF16)] * 3
    extra = [((NY * TOK, BLK), BF16), ((2, BLK, COLS), BF16)]
    *kv_parts, xt, wkv = call(
        proj_kv_body, [block_input, *t, *o, *kv_pieces], [ANY] + [VM] * 14,
        part_shapes + extra, [pltpu.SemaphoreType.DMA])
    kv_in = y_reduce(kv_parts)
    kv = (kv_parts[0] + sum(r.astype(F32) for r in kv_in)).astype(BF16)
    kv_lo = lax.ppermute(kv, ("y", "z"), ahead)
    kv_hi = lax.ppermute(kv, ("y", "z"), behind)

    *qo_parts, gt, wqo = call(
        proj_qo_body, [grad_output, xt, *t, *o, *qo_pieces], [ANY] + [VM] * 15,
        part_shapes + extra, [pltpu.SemaphoreType.DMA])
    qo_in = y_reduce(qo_parts)

    qa, kv_own, to_lo, to_hi = call(
        attend_body, [clip_ids, kv, kv_lo, kv_hi, qo_parts[0], *qo_in], [SM] + [VM] * 7,
        [((TOK, BLK), BF16), ((TOK, BLK), F32), ((TOK, BLK), BF16), ((TOK, BLK), BF16)])
    from_hi = lax.ppermute(to_lo, ("y", "z"), behind)
    from_lo = lax.ppermute(to_hi, ("y", "z"), ahead)
    qa_all = y_gather(qa)
    gkv = (kv_own + from_lo.astype(F32) + from_hi.astype(F32)).astype(BF16)
    kv_all = y_gather(gkv)

    slab_shapes = [((2, SLAB, COLS), F32)] + [((2, SLAB, COLS), BF16)] * 7
    acc = [pltpu.VMEM((2, BLK, COLS), F32)]
    slabs_qo = call(weight_grad_body, [xt, gt, *qa_all], [VM] * 6, slab_shapes, acc)
    grad_qo = z_reduce(slabs_qo)
    slabs_kv = call(weight_grad_body, [xt, xt, *kv_all], [VM] * 6, slab_shapes, acc)
    grad_kv = z_reduce(slabs_kv)

    keep, send = call(
        input_grad_body, [wkv, wqo, *qa_all, *kv_all], [VM] * 10,
        [((NY, TOK, COLS), F32), ((NY, TOK, COLS), BF16)],
        [pltpu.VMEM((2, NY, TOK, COLS), F32)])
    both = (keep + lax.ppermute(send, "c", cyc(2, 1)).astype(F32)).astype(BF16)
    total = jnp.zeros((TOK, COLS), F32)
    for j in range(NY):
        pairs = [(a * NX + b, ((b + j) % NY) * NX + a) for a in range(NY) for b in range(NX)]
        total = total + lax.ppermute(both[j], ("y", "x"), pairs).astype(F32)
    grad_weights = jnp.stack([grad_qo[0], grad_kv[0], grad_kv[1], grad_qo[1]], axis=1)
    return total.astype(BF16), grad_weights


def solution(mesh):
    torus = Mesh(mesh.devices.reshape(NY, NZ, NX, 2), ("y", "z", "x", "c"))
    seq, head = ("y", "z"), ("x", "c")
    return jax.shard_map(
        on_device,
        mesh=torus,
        in_specs=(P(seq, None), P(seq, None), P(seq, None, head), P()),
        out_specs=(P(seq, head), P(seq, None, head)),
        check_vma=False,
    )
```

```python
import functools

import jax
import jax.numpy as jnp
from jax import lax
from jax.experimental import pallas as pl
from jax.experimental.pallas import tpu as pltpu
from jax.sharding import Mesh
from jax.sharding import PartitionSpec as P

F32 = jnp.float32
BF16 = jnp.bfloat16
HD = 128
NY, NZ, NX = 4, 8, 4
TOK = 128
COLS = 384
BLK = 768
SLAB = 96


VM = pl.BlockSpec(memory_space=pltpu.VMEM)
ANY = pl.BlockSpec(memory_space=pl.ANY)
SM = pl.BlockSpec(memory_space=pltpu.SMEM)


def sds(shape, dtype):
    return jax.ShapeDtypeStruct(shape, dtype)


def mm(a, b, ca, cb):
    return lax.dot_general(a, b, (((ca,), (cb,)), ((), ())), preferred_element_type=F32)


def cyc(n, k):
    return [(i, (i + k) % n) for i in range(n)]


def params():
    return pltpu.CompilerParams(vmem_limit_bytes=20 * 2**20)


def gather_weights(refs, wfull):
    z = lax.axis_index("z")
    for j, ref in enumerate(refs):
        shift = -j if j <= 4 else j - 4
        start = pl.multiple_of(lax.rem(z + shift + NZ, NZ) * SLAB, 32)
        wfull[:, pl.ds(start, SLAB), :] = ref[...]


def put_partials(part, s, outs):
    outs[0][:, s * COLS : (s + 1) * COLS] = part[:TOK]
    for k in range(1, NY):
        outs[k][:, s * COLS : (s + 1) * COLS] = part[k * TOK : (k + 1) * TOK].astype(BF16)


def proj_kv_body(x_hbm, *refs):
    t, o, w = refs[0:3], refs[3:6], refs[6:14]
    outs, xt, wfull, sem = refs[14:18], refs[18], refs[19], refs[20]
    y, c = lax.axis_index("y"), lax.axis_index("c")
    own = pltpu.make_async_copy(
        x_hbm.at[:, pl.ds(pl.multiple_of(y * BLK, BLK), BLK)], xt.at[pl.ds(0, TOK), :], sem
    )
    own.start()
    gather_weights(w, wfull)
    for k in range(1, NY):
        xt[k * TOK : (k + 1) * TOK, :] = jnp.where(c == 0, t[k - 1][...], o[k - 1][...])
    own.wait()
    rows = xt[...]
    for s in range(2):
        put_partials(mm(rows, wfull[s], 1, 0), s, outs)


def proj_qo_body(g_hbm, xt, *refs):
    t, o, w = refs[0:3], refs[3:6], refs[6:14]
    outs, gt, wfull, sem = refs[14:18], refs[18], refs[19], refs[20]
    y, c = lax.axis_index("y"), lax.axis_index("c")
    own = pltpu.make_async_copy(
        g_hbm.at[:, pl.ds(pl.multiple_of(y * BLK, BLK), BLK)], gt.at[pl.ds(0, TOK), :], sem
    )
    own.start()
    gather_weights(w, wfull)
    for k in range(1, NY):
        gt[k * TOK : (k + 1) * TOK, :] = jnp.where(c == 0, o[k - 1][...], t[k - 1][...])
    put_partials(mm(xt[...], wfull[0], 1, 0), 0, outs)
    own.wait()
    put_partials(mm(gt[...], wfull[1], 1, 0), 1, outs)


def attend_body(clip, kv, kv_lo, kv_hi, own, r1, r2, r3, out_qa, out_own, out_lo, out_hi):
    s_idx = lax.axis_index("y") * NZ + lax.axis_index("z")
    last = NY * NZ - 1
    mine = clip[s_idx]
    ok_lo = jnp.logical_and(s_idx > 0, clip[jnp.maximum(s_idx - 1, 0)] == mine)
    ok_hi = jnp.logical_and(s_idx < last, clip[jnp.minimum(s_idx + 1, last)] == mine)
    col = lax.broadcasted_iota(jnp.int32, (TOK, 3 * TOK), 1)
    allowed = jnp.where(
        col < TOK,
        ok_lo.astype(jnp.int32),
        jnp.where(col < 2 * TOK, 1, ok_hi.astype(jnp.int32)),
    ) > 0
    scale = HD**-0.5
    qg = (
        own[...] + r1[...].astype(F32) + r2[...].astype(F32) + r3[...].astype(F32)
    ).astype(BF16)
    for h in range(3):
        a, b = h * HD, COLS + h * HD
        q, g = qg[:, a : a + HD], qg[:, b : b + HD]
        k3 = jnp.concatenate([r[:, a : a + HD] for r in (kv_lo, kv, kv_hi)], axis=0)
        v3 = jnp.concatenate([r[:, b : b + HD] for r in (kv_lo, kv, kv_hi)], axis=0)
        scores = jnp.where(allowed, mm(q, k3, 1, 1) * scale, -1e30)
        top = jnp.max(scores, axis=1, keepdims=True)
        expo = jnp.where(allowed, jnp.exp(scores - top), 0.0)
        prob = expo / jnp.sum(expo, axis=1, keepdims=True)
        low = prob.astype(BF16)
        attn = mm(low, v3, 1, 0)
        delta = jnp.sum(g.astype(F32) * attn, axis=1, keepdims=True)
        ds = (prob * (mm(g, v3, 1, 1) - delta)).astype(BF16)
        out_qa[:, a : a + HD] = (mm(ds, k3, 1, 0) * scale).astype(BF16)
        out_qa[:, b : b + HD] = attn.astype(BF16)
        gk = mm(ds, q, 0, 0) * scale
        gv = mm(low, g, 0, 0)
        for at, val in ((a, gk), (b, gv)):
            out_lo[:, at : at + HD] = val[:TOK].astype(BF16)
            out_own[:, at : at + HD] = val[TOK : 2 * TOK]
            out_hi[:, at : at + HD] = val[2 * TOK :].astype(BF16)


def weight_grad_body(xt, gt, g0, g1, g2, g3, *refs):
    outs, acc = refs[:NZ], refs[NZ]
    z = lax.axis_index("z")
    for s, at, rows in ((0, 0, xt), (3, 1, gt), (1, 2, xt), (2, 3, xt)):
        cols = jnp.concatenate([r[:, at * COLS : (at + 1) * COLS] for r in (g0, g1, g2, g3)], axis=0)
        acc[...] = mm(rows[...], cols, 0, 0)
        for j in range(NZ):
            start = pl.multiple_of(lax.rem(z + j, NZ) * SLAB, 32)
            outs[j][s] = acc[pl.ds(start, SLAB), :].astype(outs[j].dtype)


def input_grad_body(wkv, wqo, *refs):
    grads, out, acc, cols = refs[0:4], refs[4], refs[5], refs[6]
    y = lax.axis_index("y")
    for b, ref in enumerate(grads):
        rows = pl.ds(b * TOK, TOK)
        for k, at in enumerate((0, 2, 3)):
            cols[k, rows, :] = ref[:, at * COLS : (at + 1) * COLS]

    def part(i, carry):
        d = pl.ds(pl.multiple_of(i * COLS, COLS), COLS)
        total = (
            mm(cols[0], wqo[0, d, :], 1, 1)
            + mm(cols[1], wkv[0, d, :], 1, 1)
            + mm(cols[2], wkv[1, d, :], 1, 1)
        )
        acc[i] = total.reshape(NY, TOK, COLS).astype(BF16)
        return carry

    lax.fori_loop(0, 2, part, 0)
    for a in range(NY):
        b = lax.rem(y - a + NY, NY)
        for i in range(2):
            out[2 * a + i] = acc[i, b]


def call(body, ins, specs, outs, scratch=()):
    return pl.pallas_call(
        body,
        in_specs=specs,
        out_specs=[VM] * len(outs),
        out_shape=[sds(*o) for o in outs],
        scratch_shapes=list(scratch),
        compiler_params=params(),
    )(*ins)


def z_gather(w):
    right, left = [w], []
    for k in range(4):
        right.append(lax.ppermute(right[-1], "z", cyc(NZ, 1)))
        if k < 3:
            left.append(lax.ppermute(left[-1] if left else w, "z", cyc(NZ, -1)))
    return right + left


def far_pairs():
    return [
        (i * 2 + k, (i + (2 if k == 0 else -2)) % NZ * 2 + k) for i in range(NZ) for k in range(2)
    ]


def z_reduce(slabs, even):
    up3 = lax.ppermute(slabs[3], "z", cyc(NZ, 1)).astype(F32)
    down3 = lax.ppermute(slabs[5], "z", cyc(NZ, -1)).astype(F32)
    far = lax.ppermute(slabs[4], ("z", "c"), far_pairs()).astype(F32)
    up1 = lax.ppermute(slabs[1], "z", cyc(NZ, 1))
    down1 = lax.ppermute(slabs[7], "z", cyc(NZ, -1))
    up = slabs[2].astype(F32) + up3 + jnp.where(even, far, 0.0)
    down = slabs[6].astype(F32) + down3 + jnp.where(even, 0.0, far)
    up2 = lax.ppermute(up.astype(BF16), "z", cyc(NZ, 2))
    down2 = lax.ppermute(down.astype(BF16), "z", cyc(NZ, -2))
    total = slabs[0] + up1.astype(F32) + down1.astype(F32) + up2.astype(F32) + down2.astype(F32)
    return total.astype(BF16)


def y_reduce(parts):
    return [lax.ppermute(parts[k], "y", cyc(NY, -k)) for k in range(1, NY)]


def y_gather(rows):
    return [rows] + [lax.ppermute(rows, "y", cyc(NY, k)) for k in range(1, NY)]


def on_device(block_input, grad_output, weights, clip_ids):
    y, c = lax.axis_index("y"), lax.axis_index("c")
    frames = NY * NZ
    ahead = [(i, i + 1) for i in range(frames - 1)]
    behind = [(i + 1, i) for i in range(frames - 1)]
    w_t = jnp.transpose(weights, (1, 0, 2))
    kv_pieces = z_gather(w_t[1:3])
    qo_pieces = z_gather(jnp.stack([w_t[0], w_t[3]]))
    t = []
    for k in range(1, NY):
        start = lax.rem(y + k, NY) * BLK
        piece = jnp.where(
            c == 0,
            lax.dynamic_slice_in_dim(block_input, start, BLK, 1),
            lax.dynamic_slice_in_dim(grad_output, start, BLK, 1),
        )
        t.append(lax.ppermute(piece, "y", cyc(NY, k)))
    o = [lax.ppermute(piece, "c", cyc(2, 1)) for piece in t]

    part_shapes = [((TOK, BLK), F32)] + [((TOK, BLK), BF16)] * 3
    extra = [((NY * TOK, BLK), BF16), ((2, BLK, COLS), BF16)]
    *kv_parts, xt, wkv = call(
        proj_kv_body, [block_input, *t, *o, *kv_pieces], [ANY] + [VM] * 14,
        part_shapes + extra, [pltpu.SemaphoreType.DMA])
    kv_in = y_reduce(kv_parts)
    kv = (kv_parts[0] + sum(r.astype(F32) for r in kv_in)).astype(BF16)
    kv_lo = lax.ppermute(kv, ("y", "z"), ahead)
    kv_hi = lax.ppermute(kv, ("y", "z"), behind)

    *qo_parts, gt, wqo = call(
        proj_qo_body, [grad_output, xt, *t, *o, *qo_pieces], [ANY] + [VM] * 15,
        part_shapes + extra, [pltpu.SemaphoreType.DMA])
    qo_in = y_reduce(qo_parts)

    qa, kv_own, to_lo, to_hi = call(
        attend_body, [clip_ids, kv, kv_lo, kv_hi, qo_parts[0], *qo_in], [SM] + [VM] * 7,
        [((TOK, BLK), BF16), ((TOK, BLK), F32), ((TOK, BLK), BF16), ((TOK, BLK), BF16)])
    from_hi = lax.ppermute(to_lo, ("y", "z"), behind)
    from_lo = lax.ppermute(to_hi, ("y", "z"), ahead)
    gkv = (kv_own + from_lo.astype(F32) + from_hi.astype(F32)).astype(BF16)
    grads = y_gather(jnp.concatenate([qa, gkv], axis=1))

    slabs = call(
        weight_grad_body, [xt, gt, *grads], [VM] * 6,
        [((4, SLAB, COLS), F32)] + [((4, SLAB, COLS), BF16)] * 7, [pltpu.VMEM((BLK, COLS), F32)])
    grad_weights = jnp.transpose(z_reduce(slabs, c == 0), (1, 0, 2))

    (partial_input,) = call(
        input_grad_body, [wkv, wqo, *grads], [VM] * 6, [((2 * NX, TOK, COLS), BF16)],
        [pltpu.VMEM((2, NY, TOK, COLS), BF16), pltpu.VMEM((3, NY * TOK, COLS), BF16)])
    seen = lax.all_to_all(partial_input, ("x", "c"), split_axis=0, concat_axis=0, tiled=True)
    total = jnp.sum(seen.astype(F32), axis=0).astype(BF16)
    pairs = [(a * NX + b, b * NX + a) for a in range(NY) for b in range(NX)]
    return lax.ppermute(total, ("y", "x"), pairs), grad_weights


def solution(mesh):
    torus = Mesh(mesh.devices.reshape(NY, NZ, NX, 2), ("y", "z", "x", "c"))
    seq, head = ("y", "z"), ("x", "c")
    return jax.shard_map(
        on_device,
        mesh=torus,
        in_specs=(P(seq, None), P(seq, None), P(seq, None, head), P()),
        out_specs=(P(seq, head), P(seq, None, head)),
        check_vma=False,
    )
```

```python
import functools

import jax
import jax.numpy as jnp
from jax import lax
from jax.experimental import pallas as pl
from jax.experimental.pallas import tpu as pltpu
from jax.sharding import Mesh
from jax.sharding import PartitionSpec as P

F32 = jnp.float32
BF16 = jnp.bfloat16
HD = 128
NY, NZ, NX = 4, 8, 4
TOK = 128
COLS = 384
BLK = 768
SLAB = 96


VM = pl.BlockSpec(memory_space=pltpu.VMEM)
ANY = pl.BlockSpec(memory_space=pl.ANY)
SM = pl.BlockSpec(memory_space=pltpu.SMEM)


def sds(shape, dtype):
    return jax.ShapeDtypeStruct(shape, dtype)


def mm(a, b, ca, cb):
    return lax.dot_general(a, b, (((ca,), (cb,)), ((), ())), preferred_element_type=F32)


def cyc(n, k):
    return [(i, (i + k) % n) for i in range(n)]


def params():
    return pltpu.CompilerParams(vmem_limit_bytes=20 * 2**20)


def gather_weights(refs, wfull):
    z = lax.axis_index("z")
    for j, ref in enumerate(refs):
        shift = -j if j <= 4 else j - 4
        start = pl.multiple_of(lax.rem(z + shift + NZ, NZ) * SLAB, 32)
        wfull[:, pl.ds(start, SLAB), :] = ref[...]


def put_partials(part, s, outs):
    outs[0][:, s * COLS : (s + 1) * COLS] = part[:TOK]
    for k in range(1, NY):
        outs[k][:, s * COLS : (s + 1) * COLS] = part[k * TOK : (k + 1) * TOK].astype(BF16)


def proj_kv_body(x_hbm, *refs):
    t, w = refs[0:3], refs[3:11]
    outs, xt, wfull, sem = refs[11:15], refs[15], refs[16], refs[17]
    y = lax.axis_index("y")
    own = pltpu.make_async_copy(
        x_hbm.at[:, pl.ds(pl.multiple_of(y * BLK, BLK), BLK)], xt.at[pl.ds(0, TOK), :], sem
    )
    own.start()
    gather_weights(w, wfull)
    for k in range(1, NY):
        xt[k * TOK : (k + 1) * TOK, :] = t[k - 1][0]
    own.wait()
    rows = xt[...]
    for s in range(2):
        put_partials(mm(rows, wfull[s], 1, 0), s, outs)


def proj_qo_body(g_hbm, xt, *refs):
    t, w = refs[0:3], refs[3:11]
    outs, gt, wfull, sem = refs[11:15], refs[15], refs[16], refs[17]
    y = lax.axis_index("y")
    own = pltpu.make_async_copy(
        g_hbm.at[:, pl.ds(pl.multiple_of(y * BLK, BLK), BLK)], gt.at[pl.ds(0, TOK), :], sem
    )
    own.start()
    gather_weights(w, wfull)
    for k in range(1, NY):
        gt[k * TOK : (k + 1) * TOK, :] = t[k - 1][1]
    put_partials(mm(xt[...], wfull[0], 1, 0), 0, outs)
    own.wait()
    put_partials(mm(gt[...], wfull[1], 1, 0), 1, outs)


def attend_body(clip, kv, kv_lo, kv_hi, own, r1, r2, r3, out_qa, out_own, out_lo, out_hi):
    s_idx = lax.axis_index("y") * NZ + lax.axis_index("z")
    last = NY * NZ - 1
    mine = clip[s_idx]
    ok_lo = jnp.logical_and(s_idx > 0, clip[jnp.maximum(s_idx - 1, 0)] == mine)
    ok_hi = jnp.logical_and(s_idx < last, clip[jnp.minimum(s_idx + 1, last)] == mine)
    col = lax.broadcasted_iota(jnp.int32, (TOK, 3 * TOK), 1)
    allowed = jnp.where(
        col < TOK,
        ok_lo.astype(jnp.int32),
        jnp.where(col < 2 * TOK, 1, ok_hi.astype(jnp.int32)),
    ) > 0
    scale = HD**-0.5
    qg = (
        own[...] + r1[...].astype(F32) + r2[...].astype(F32) + r3[...].astype(F32)
    ).astype(BF16)
    for h in range(3):
        a, b = h * HD, COLS + h * HD
        q, g = qg[:, a : a + HD], qg[:, b : b + HD]
        k3 = jnp.concatenate([r[:, a : a + HD] for r in (kv_lo, kv, kv_hi)], axis=0)
        v3 = jnp.concatenate([r[:, b : b + HD] for r in (kv_lo, kv, kv_hi)], axis=0)
        scores = jnp.where(allowed, mm(q, k3, 1, 1) * scale, -1e30)
        top = jnp.max(scores, axis=1, keepdims=True)
        expo = jnp.where(allowed, jnp.exp(scores - top), 0.0)
        prob = expo / jnp.sum(expo, axis=1, keepdims=True)
        low = prob.astype(BF16)
        attn = mm(low, v3, 1, 0)
        delta = jnp.sum(g.astype(F32) * attn, axis=1, keepdims=True)
        ds = (prob * (mm(g, v3, 1, 1) - delta)).astype(BF16)
        out_qa[:, a : a + HD] = (mm(ds, k3, 1, 0) * scale).astype(BF16)
        out_qa[:, b : b + HD] = attn.astype(BF16)
        gk = mm(ds, q, 0, 0) * scale
        gv = mm(low, g, 0, 0)
        for at, val in ((a, gk), (b, gv)):
            out_lo[:, at : at + HD] = val[:TOK].astype(BF16)
            out_own[:, at : at + HD] = val[TOK : 2 * TOK]
            out_hi[:, at : at + HD] = val[2 * TOK :].astype(BF16)


def weight_grad_body(xt, gt, g0, g1, g2, g3, *refs):
    outs, acc = refs[:NZ], refs[NZ]
    z = lax.axis_index("z")
    for s, at, rows in ((0, 0, xt), (3, 1, gt), (1, 2, xt), (2, 3, xt)):
        cols = jnp.concatenate([r[:, at * COLS : (at + 1) * COLS] for r in (g0, g1, g2, g3)], axis=0)
        acc[...] = mm(rows[...], cols, 0, 0)
        for j in range(NZ):
            start = pl.multiple_of(lax.rem(z + j, NZ) * SLAB, 32)
            outs[j][s] = acc[pl.ds(start, SLAB), :].astype(outs[j].dtype)


def input_grad_body(wkv, wqo, *refs):
    grads, out, acc, cols = refs[0:4], refs[4], refs[5], refs[6]
    y = lax.axis_index("y")
    for b, ref in enumerate(grads):
        rows = pl.ds(b * TOK, TOK)
        for k, at in enumerate((0, 2, 3)):
            cols[k, rows, :] = ref[:, at * COLS : (at + 1) * COLS]

    def part(i, carry):
        d = pl.ds(pl.multiple_of(i * COLS, COLS), COLS)
        total = (
            mm(cols[0], wqo[0, d, :], 1, 1)
            + mm(cols[1], wkv[0, d, :], 1, 1)
            + mm(cols[2], wkv[1, d, :], 1, 1)
        )
        acc[i] = total.reshape(NY, TOK, COLS).astype(BF16)
        return carry

    lax.fori_loop(0, 2, part, 0)
    for a in range(NY):
        b = lax.rem(y - a + NY, NY)
        for i in range(2):
            out[2 * a + i] = acc[i, b]


def call(body, ins, specs, outs, scratch=()):
    return pl.pallas_call(
        body,
        in_specs=specs,
        out_specs=[VM] * len(outs),
        out_shape=[sds(*o) for o in outs],
        scratch_shapes=list(scratch),
        compiler_params=params(),
    )(*ins)


def z_gather(w):
    right, left = [w], []
    for k in range(4):
        right.append(lax.ppermute(right[-1], "z", cyc(NZ, 1)))
        if k < 3:
            left.append(lax.ppermute(left[-1] if left else w, "z", cyc(NZ, -1)))
    return right + left


def far_pairs():
    return [
        (i * 2 + k, (i + (2 if k == 0 else -2)) % NZ * 2 + k) for i in range(NZ) for k in range(2)
    ]


def z_reduce(slabs, even):
    up3 = lax.ppermute(slabs[3], "z", cyc(NZ, 1)).astype(F32)
    down3 = lax.ppermute(slabs[5], "z", cyc(NZ, -1)).astype(F32)
    far = lax.ppermute(slabs[4], ("z", "c"), far_pairs()).astype(F32)
    up1 = lax.ppermute(slabs[1], "z", cyc(NZ, 1))
    down1 = lax.ppermute(slabs[7], "z", cyc(NZ, -1))
    up = slabs[2].astype(F32) + up3 + jnp.where(even, far, 0.0)
    down = slabs[6].astype(F32) + down3 + jnp.where(even, 0.0, far)
    up2 = lax.ppermute(up.astype(BF16), "z", cyc(NZ, 2))
    down2 = lax.ppermute(down.astype(BF16), "z", cyc(NZ, -2))
    total = slabs[0] + up1.astype(F32) + down1.astype(F32) + up2.astype(F32) + down2.astype(F32)
    return total.astype(BF16)


def y_reduce(parts):
    return [lax.ppermute(parts[k], "y", cyc(NY, -k)) for k in range(1, NY)]


def y_gather(rows):
    return [rows] + [lax.ppermute(rows, "y", cyc(NY, k)) for k in range(1, NY)]


def on_device(block_input, grad_output, weights, clip_ids):
    y, c = lax.axis_index("y"), lax.axis_index("c")
    frames = NY * NZ
    ahead = [(i, i + 1) for i in range(frames - 1)]
    behind = [(i + 1, i) for i in range(frames - 1)]
    w_t = jnp.transpose(weights, (1, 0, 2))
    kv_pieces = z_gather(w_t[1:3])
    qo_pieces = z_gather(jnp.stack([w_t[0], w_t[3]]))
    t = []
    for k in range(1, NY):
        start = lax.rem(y + k, NY) * BLK
        piece = jnp.stack(
            [lax.dynamic_slice_in_dim(v, start, BLK, 1) for v in (block_input, grad_output)]
        )
        t.append(lax.ppermute(piece, "y", cyc(NY, k)))

    part_shapes = [((TOK, BLK), F32)] + [((TOK, BLK), BF16)] * 3
    extra = [((NY * TOK, BLK), BF16), ((2, BLK, COLS), BF16)]
    *kv_parts, xt, wkv = call(
        proj_kv_body, [block_input, *t, *kv_pieces], [ANY] + [VM] * 11,
        part_shapes + extra, [pltpu.SemaphoreType.DMA])
    kv_in = y_reduce(kv_parts)
    kv = (kv_parts[0] + sum(r.astype(F32) for r in kv_in)).astype(BF16)
    kv_lo = lax.ppermute(kv, ("y", "z"), ahead)
    kv_hi = lax.ppermute(kv, ("y", "z"), behind)

    *qo_parts, gt, wqo = call(
        proj_qo_body, [grad_output, xt, *t, *qo_pieces], [ANY] + [VM] * 12,
        part_shapes + extra, [pltpu.SemaphoreType.DMA])
    qo_in = y_reduce(qo_parts)

    qa, kv_own, to_lo, to_hi = call(
        attend_body, [clip_ids, kv, kv_lo, kv_hi, qo_parts[0], *qo_in], [SM] + [VM] * 7,
        [((TOK, BLK), BF16), ((TOK, BLK), F32), ((TOK, BLK), BF16), ((TOK, BLK), BF16)])
    from_hi = lax.ppermute(to_lo, ("y", "z"), behind)
    from_lo = lax.ppermute(to_hi, ("y", "z"), ahead)
    gkv = (kv_own + from_lo.astype(F32) + from_hi.astype(F32)).astype(BF16)
    grads = y_gather(jnp.concatenate([qa, gkv], axis=1))

    slabs = call(
        weight_grad_body, [xt, gt, *grads], [VM] * 6,
        [((4, SLAB, COLS), F32)] + [((4, SLAB, COLS), BF16)] * 7, [pltpu.VMEM((BLK, COLS), F32)])
    grad_weights = jnp.transpose(z_reduce(slabs, c == 0), (1, 0, 2))

    (partial_input,) = call(
        input_grad_body, [wkv, wqo, *grads], [VM] * 6, [((2 * NX, TOK, COLS), BF16)],
        [pltpu.VMEM((2, NY, TOK, COLS), BF16), pltpu.VMEM((3, NY * TOK, COLS), BF16)])
    seen = lax.all_to_all(partial_input, ("x", "c"), split_axis=0, concat_axis=0, tiled=True)
    total = jnp.sum(seen.astype(F32), axis=0).astype(BF16)
    pairs = [(a * NX + b, b * NX + a) for a in range(NY) for b in range(NX)]
    return lax.ppermute(total, ("y", "x"), pairs), grad_weights


def solution(mesh):
    torus = Mesh(mesh.devices.reshape(NY, NZ, NX, 2), ("y", "z", "x", "c"))
    seq, head = ("y", "z"), ("x", "c")
    return jax.shard_map(
        on_device,
        mesh=torus,
        in_specs=(P(seq, None), P(seq, None), P(seq, None, head), P()),
        out_specs=(P(seq, head), P(seq, None, head)),
        check_vma=False,
    )
```
